128 devices in a mesh: row: 8 (over y, core), col: 16 (over x, z).
Axes of the slice: x: 4, y: 4, z: 4, core: 2. Of those that a mesh axis runs over, the one named last changes fastest.
Arguments:
- tokens: bfloat16 [1024, 8192], P('row', 'col'), may hold values from -6 to 6
- gate_weight: bfloat16 [8192, 28672], P('col', 'row'), may hold values from -0.09375 to 0.09375
- up_weight: bfloat16 [8192, 28672], P('col', 'row'), may hold values from -0.09375 to 0.09375
- down_weight: bfloat16 [28672, 8192], P('row', 'col'), may hold values from -0.046875 to 0.046875
- gate_mask: int32 [64, 224], P('col', 'row'), may hold values 0 or 1
- up_mask: int32 [64, 224], P('col', 'row'), may hold values 0 or 1
- down_mask: int32 [224, 64], P('row', 'col'), may hold values 0 or 1
Outputs:
- mixed_out: bfloat16 [1024, 8192], P('row', 'col')
The draws below stay inside these ranges and needn't reach their ends.
Inputs may be any that keep to these rules, and one draw needn't show every extreme that they name: `gate_mask`: each entry keeps (1) or drops (0) one block. `up_mask`: each entry keeps (1) or drops (0) one block. `down_mask`: each entry keeps (1) or drops (0) one block.
All inputs are finite; a program needn't handle non-finite values.
Results may differ from the reference program's by a relative error of at most 0.025.
Values may be sent and summed in bfloat16 or wider, within the bound.
A program may use at most 128 MiB of HBM per device.

```python
import jax
import jax.numpy as jnp
from jax import lax

D = 8192
FF = 28672
BLOCK = 128
TOKENS = 1024
N_COL = 16


def place_ends(result, stream_key, least, high):
    extent = result.shape
    place = [jax.random.randint(jax.random.fold_in(stream_key, axis), (), 0, extent[axis]) for axis in range(len(extent))]
    result = result.at[tuple(place)].set(least)
    longest = extent.index(max(extent))
    place[longest] = (place[longest] + 1) % extent[longest]
    return result.at[tuple(place)].set(high)


def block_levels(key, shape, split, low, high):
    level, own = 1.0, jax.random.fold_in(key, 6)
    for dim, shards_of in split:
        draws = jnp.exp(jax.random.uniform(jax.random.fold_in(own, dim), (shards_of,), jnp.float32, low / len(split), high / len(split)))
        level = level * jnp.repeat(draws, shape[dim] // shards_of).reshape([-1 if axis == dim else 1 for axis in range(len(shape))])
    return level


def bell_draw(key, extent, deviation, limit, split=(), held_as=jnp.bfloat16):
    entries = jax.random.normal(key, extent, jnp.float32) * deviation
    if len(split) > 0:
        entries = block_levels(key, extent, split, -0.22, 0.18) * entries
    return jnp.clip(entries, min=-limit, max=limit).astype(held_as)


def setup_inputs(seed: int = 0) -> dict:
    splits = jax.random.split(jax.random.key(seed), 8)
    tokens = bell_draw(splits[0], (TOKENS, D), 1.0, 6.0, ((0, 8), (1, 16)))
    gate_weight = bell_draw(splits[1], (D, FF), (D // 2) ** -0.5, 0.09375, ((0, 16), (1, 8)))
    up_weight = bell_draw(splits[2], (D, FF), (D // 2) ** -0.5, 0.09375, ((0, 16), (1, 8)))
    down_weight = bell_draw(splits[3], (FF, D), (FF // 2) ** -0.5, 0.046875, ((0, 8), (1, 16)))
    gate_mask = place_ends((jax.random.randint(splits[4], (D // BLOCK, FF // BLOCK), 0, 2) < 1).astype(jnp.int32), jax.random.fold_in(splits[4], 1), 0, 1)
    up_mask = place_ends((jax.random.randint(splits[5], (D // BLOCK, FF // BLOCK), 0, 2) < 1).astype(jnp.int32), jax.random.fold_in(splits[5], 1), 0, 1)
    down_mask = place_ends((jax.random.randint(splits[6], (FF // BLOCK, D // BLOCK), 0, 2) < 1).astype(jnp.int32), jax.random.fold_in(splits[6], 1), 0, 1)
    return dict(tokens=tokens, gate_weight=gate_weight, up_weight=up_weight, down_weight=down_weight, gate_mask=gate_mask, up_mask=up_mask, down_mask=down_mask)


def expand(weight, block_mask):
    row_count, col_count = weight.shape
    mask_rows, mask_cols = block_mask.shape
    shaped = weight.reshape(mask_rows, row_count // mask_rows, mask_cols, col_count // mask_cols)
    kept_blocks = shaped * block_mask.astype(weight.dtype)[:, None, :, None]
    return kept_blocks.reshape(row_count, col_count)


def reference(tokens, gate_weight, up_weight, down_weight, gate_mask, up_mask, down_mask):
    kept_gate = expand(gate_weight, gate_mask)
    kept_up = expand(up_weight, up_mask)
    kept_down = expand(down_weight, down_mask)
    run_width = D // N_COL
    token_runs = tokens.reshape(TOKENS, N_COL, run_width).transpose(1, 0, 2)
    gate_runs = kept_gate.reshape(N_COL, run_width, FF)
    up_runs = kept_up.reshape(N_COL, run_width, FF)

    def add_run(totals, pieces):
        x_run, g_run, u_run = pieces
        g_part = jnp.dot(x_run, g_run, preferred_element_type=jnp.float32).astype(jnp.bfloat16)
        u_part = jnp.dot(x_run, u_run, preferred_element_type=jnp.float32).astype(jnp.bfloat16)
        g_part, u_part = lax.optimization_barrier((g_part, u_part))
        return (totals[0] + g_part.astype(jnp.float32), totals[1] + u_part.astype(jnp.float32)), None

    empty_sum = jnp.zeros((TOKENS, FF), jnp.float32)
    (gate_sum, up_sum), _ = lax.scan(add_run, (empty_sum, empty_sum), (token_runs, gate_runs, up_runs))
    hidden = (jax.nn.silu(gate_sum) * up_sum).astype(jnp.bfloat16)
    return jnp.dot(hidden, kept_down, preferred_element_type=jnp.float32).astype(jnp.bfloat16)
```

```python
import functools

import jax
import jax.numpy as jnp
from jax import lax
from jax.experimental import pallas as pl
from jax.experimental.pallas import tpu as pltpu
from jax.sharding import PartitionSpec as P

ROUNDS = 14
BLOCK = 128
LAGS = 8
F32, BF16 = jnp.float32, jnp.bfloat16
MESH = pl.DeviceIdType.MESH


def layer_kernel(
    tok_hbm, gate_hbm, up_hbm, down_hbm, gm, um, dm, out_ref,
    tok, w_gate, w_up, w_down,
    s1, r1h, r1f, part, s2, r2h, r2f, hid, acc, o_send, o_recv, oy_send, oy_h, oy_f,
    load_sem, tok_ss, tok_rs, rs_ss, rs_rs, ag_ss, ag_rs, out_ss, out_rs,
):
    cw = w_gate.shape[2]
    half_cw = cw // 2
    row, col = lax.axis_index("row"), lax.axis_index("col")
    y, core = row // 2, row % 2
    x, z = col // 4, col % 4
    coord = (x, z)

    def turn(v, k):
        return (v + k + 4) % 4

    def in_plane(axis, k):
        if axis == 0:
            return (row, turn(x, k) * 4 + z)
        return (row, x * 4 + turn(z, k))

    def in_line(k):
        return (turn(y, k) * 2 + core, col)

    twin = (row + 1 - 2 * core, col)
    step = (1, -1)

    def remote(src, dst, ss, rs, device):
        return pltpu.make_async_remote_copy(
            src_ref=src, dst_ref=dst, send_sem=ss, recv_sem=rs, device_id=device, device_id_type=MESH
        )

    def load_gate(j):
        return pltpu.make_async_copy(gate_hbm.at[:, pl.ds(pl.multiple_of(j * cw, cw), cw)], w_gate.at[j], load_sem.at[0, j])

    def load_up(j):
        return pltpu.make_async_copy(up_hbm.at[:, pl.ds(pl.multiple_of(j * cw, cw), cw)], w_up.at[j], load_sem.at[1, j])

    def load_down(j):
        return pltpu.make_async_copy(down_hbm.at[pl.ds(pl.multiple_of(j * cw, cw), cw)], w_down.at[j], load_sem.at[2, j])

    load_tok = pltpu.make_async_copy(tok_hbm, tok.at[y, pl.ds(2 * core, 2)], load_sem.at[3, 0])
    load_tok.start()

    @pl.loop(0, ROUNDS)
    def _(j):
        load_gate(j).start()
        load_up(j).start()

    @pl.loop(0, ROUNDS)
    def _(j):
        load_down(j).start()

    barrier = pltpu.get_barrier_semaphore()
    peers = [in_plane(a, k) for a in (0, 1) for k in step] + [in_line(k) for k in step] + [twin]
    for peer in peers:
        pl.semaphore_signal(barrier, inc=1, device_id=peer, device_id_type=MESH)
    pl.semaphore_wait(barrier, len(peers))

    mine = pl.ds(2 * core, 2)

    def tok_full(d):
        return remote(tok_hbm, tok.at[y, mine], tok_ss.at[d], tok_rs.at[d], in_line(step[d]))

    def tok_half(d):
        piece = tok.at[turn(y, -step[d]), 2 * core + d]
        return remote(piece, piece, tok_ss.at[2 + d], tok_rs.at[2 + d], in_line(step[d]))

    def tok_twin(k):
        piece = tok.at[turn(y, k), mine]
        return remote(piece, piece, tok_ss.at[4 + k % 4], tok_rs.at[4 + k % 4], twin)

    tok_full(0).start()
    tok_full(1).start()
    load_tok.wait()
    tok_twin(0).start()
    for d in (0, 1):
        tok_full(d).wait_recv()
        tok_half(d).start()
        tok_twin(-step[d]).start()
    for d in (0, 1):
        tok_half(d).wait_recv()
    tok_twin(2).start()
    for k in range(4):
        tok_twin(k).wait_recv()

    def rs1h(j, m, d):
        return remote(s1.at[j, m, 0, pl.ds(2 * d, 2)], r1h.at[j, m, d], rs_ss.at[m * 8 + d, j], rs_rs.at[m * 8 + d, j], in_plane(m, step[d]))

    def rs1f(j, m, d):
        k = m * 8 + 2 + d
        return remote(s1.at[j, m, 1 + d], r1f.at[j, m, d], rs_ss.at[k, j], rs_rs.at[k, j], in_plane(m, step[d]))

    def rs2h(j, m, d):
        k = m * 8 + 4 + d
        return remote(s2.at[j, m, 0, pl.ds(32 * d, 32)], r2h.at[j, m, d], rs_ss.at[k, j], rs_rs.at[k, j], in_plane(1 - m, step[d]))

    def rs2f(j, m, d):
        k = m * 8 + 6 + d
        return remote(s2.at[j, m, 1 + d], r2f.at[j, m, d], rs_ss.at[k, j], rs_rs.at[k, j], in_plane(1 - m, step[d]))

    def ag1f(j, t, d):
        k = t * 8 + d
        piece = hid.at[j, t, x, z]
        return remote(piece, piece, ag_ss.at[k, j], ag_rs.at[k, j], in_plane(t, step[d]))

    def ag1h(j, t, d):
        k = t * 8 + 2 + d
        half = pl.ds(32 * d, 32)
        piece = hid.at[j, 0, turn(x, -step[d]), z, half] if t == 0 else hid.at[j, 1, x, turn(z, -step[d]), half]
        return remote(piece, piece, ag_ss.at[k, j], ag_rs.at[k, j], in_plane(t, step[d]))

    def ag2f(j, t, d):
        k = t * 8 + 4 + d
        piece = hid.at[j, 0, :, z] if t == 0 else hid.at[j, 1, x]
        return remote(piece, piece, ag_ss.at[k, j], ag_rs.at[k, j], in_plane(1 - t, step[d]))

    def ag2h(j, t, d):
        k = t * 8 + 6 + d
        half = pl.ds(32 * d, 32)
        piece = hid.at[j, 0, :, turn(z, -step[d]), half] if t == 0 else hid.at[j, 1, turn(x, -step[d]), :, half]
        return remote(piece, piece, ag_ss.at[k, j], ag_rs.at[k, j], in_plane(1 - t, step[d]))

    copies = (rs1h, rs1f, rs2h, rs2f, ag1f, ag1h, ag2f, ag2h)
    weights = (w_gate, w_up)

    def prune(w, j, mask, rows_of):
        for a in range(w.shape[1] // BLOCK):
            for b in range(w.shape[2] // BLOCK):
                keep = rows_of(a, b)
                keep = jnp.full((16, BLOCK), mask[keep[0], keep[1]].astype(F32), F32).astype(BF16)
                view = (j, pl.ds(a * BLOCK, BLOCK), pl.ds(b * BLOCK, BLOCK))
                w[view] = (w[view].reshape(BLOCK // 16, 16, BLOCK) * keep[None]).reshape(BLOCK, BLOCK)

    def product(j, m, dest):
        lhs = tok[dest] if m == 0 else tok[:, dest]
        k = lhs.shape[-1]
        return jnp.dot(lhs.reshape(256, k), weights[m][j], preferred_element_type=F32).reshape(4, 64, cw)

    def stage_a(j):
        load_gate(j).wait()
        load_up(j).wait()
        prune(w_gate, j, gm, lambda a, b: (a, j * (cw // BLOCK) + b))
        prune(w_up, j, um, lambda a, b: (a, j * (cw // BLOCK) + b))
        for m in (0, 1):
            s1[j, m, 0] = product(j, m, turn(coord[m], 2)).astype(BF16)
            for d in (0, 1):
                rs1h(j, m, d).start()

    def stage_b(j):
        for m in (0, 1):
            for d in (0, 1):
                got = product(j, m, turn(coord[m], step[d]))
                rs1h(j, m, d).wait_recv()
                s1[j, m, 1 + d, pl.ds(2 * d, 2)] = (got[2 * d : 2 * d + 2] + r1h[j, m, d].astype(F32)).astype(BF16)
                s1[j, m, 1 + d, pl.ds(2 - 2 * d, 2)] = got[2 - 2 * d : 4 - 2 * d].astype(BF16)
                rs1f(j, m, d).start()

    def stage_c(j):
        slot = j % 4
        for m in (0, 1):
            got = product(j, m, coord[m])
            rs1f(j, m, 0).wait_recv()
            rs1f(j, m, 1).wait_recv()
            part[slot, m] = got + r1f[j, m, 0].astype(F32) + r1f[j, m, 1].astype(F32)
            s2[j, m, 0] = part[slot, m, turn(coord[1 - m], 2)].astype(BF16)
            for d in (0, 1):
                rs2h(j, m, d).start()

    def stage_d(j):
        slot = j % 4
        for m in (0, 1):
            for d in (0, 1):
                rs2h(j, m, d).wait_recv()
                got = part[slot, m, turn(coord[1 - m], step[d])]
                lo, hi = 32 * d, 32 - 32 * d
                s2[j, m, 1 + d, pl.ds(lo, 32)] = (got[lo : lo + 32] + r2h[j, m, d].astype(F32)).astype(BF16)
                s2[j, m, 1 + d, pl.ds(hi, 32)] = got[hi : hi + 32].astype(BF16)
                rs2f(j, m, d).start()

    def stage_e(j):
        slot = j % 4
        for m in (0, 1):
            for d in (0, 1):
                rs2f(j, m, d).wait_recv()
        g = part[slot, 0, z] + r2f[j, 0, 0].astype(F32) + r2f[j, 0, 1].astype(F32)
        u = part[slot, 1, x] + r2f[j, 1, 0].astype(F32) + r2f[j, 1, 1].astype(F32)
        h = (g / (1.0 + jnp.exp(-g)) * u).astype(BF16)
        hid[j, 0, x, z] = h[:, :half_cw]
        hid[j, 1, x, z] = h[:, half_cw:]
        for t in (0, 1):
            for d in (0, 1):
                ag1f(j, t, d).start()

    def relay(first, then):
        def stage(j):
            for t in (0, 1):
                for d in (0, 1):
                    first(j, t, d).wait_recv()
                    then(j, t, d).start()
        return stage

    def stage_g(j):
        for t in (0, 1):
            for d in (0, 1):
                ag1h(j, t, d).wait_recv()
            for d in (0, 1):
                ag2f(j, t, d).start()

    def stage_i(j):
        load_down(j).wait()
        prune(w_down, j, dm, lambda a, b: (j * (cw // BLOCK) + a, b))
        for t in (0, 1):
            for d in (0, 1):
                ag2h(j, t, d).wait_recv()
        for q in range(4):
            lhs = jnp.concatenate([hid[j, 0, q].reshape(256, half_cw), hid[j, 1, q].reshape(256, half_cw)], axis=1)
            got = jnp.dot(lhs, w_down[j], preferred_element_type=F32).reshape(2, 128, acc.shape[-1])
            acc[pl.ds(2 * q, 2)] = acc[pl.ds(2 * q, 2)] + got

    acc[...] = jnp.zeros_like(acc)
    stages = (stage_a, stage_b, stage_c, stage_d, stage_e, relay(ag1f, ag1h), stage_g, relay(ag2f, ag2h), stage_i)

    @pl.loop(0, ROUNDS + LAGS)
    def _(i):
        for lag, stage in enumerate(stages):
            @pl.when((i >= lag) & (i < ROUNDS + lag))
            def _(stage=stage, lag=lag):
                stage(i - lag)

    def o_twin(k):
        return remote(o_send.at[k], o_recv.at[k], out_ss.at[k], out_rs.at[k], twin)

    def oyh(d):
        return remote(oy_send.at[0, pl.ds(64 * d, 64)], oy_h.at[d], out_ss.at[4 + d], out_rs.at[4 + d], in_line(step[d]))

    def oyf(d):
        return remote(oy_send.at[1 + d], oy_f.at[d], out_ss.at[6 + d], out_rs.at[6 + d], in_line(step[d]))

    order = (2, 1, 3, 0)
    for k in order:
        o_send[k] = acc[turn(y, k) * 2 + 1 - core].astype(BF16)
        o_twin(k).start()

    def paired(k):
        o_twin(k).wait_recv()
        return acc[turn(y, k) * 2 + core] + o_recv[k].astype(F32)

    oy_send[0] = paired(2).astype(BF16)
    oyh(0).start()
    oyh(1).start()
    for d in (0, 1):
        got = paired(1 if d == 0 else 3)
        oyh(d).wait_recv()
        lo, hi = 64 * d, 64 - 64 * d
        oy_send[1 + d, pl.ds(lo, 64)] = (got[lo : lo + 64] + oy_h[d].astype(F32)).astype(BF16)
        oy_send[1 + d, pl.ds(hi, 64)] = got[hi : hi + 64].astype(BF16)
        oyf(d).start()
    got = paired(0)
    oyf(0).wait_recv()
    oyf(1).wait_recv()
    out_ref[...] = (got + oy_f[0].astype(F32) + oy_f[1].astype(F32)).astype(BF16)

    for d in (0, 1):
        tok_full(d).wait_send()
        tok_half(d).wait_send()
        oyh(d).wait_send()
        oyf(d).wait_send()
    for k in range(4):
        tok_twin(k).wait_send()
        o_twin(k).wait_send()

    @pl.loop(0, ROUNDS)
    def _(j):
        for copy in copies:
            for m in (0, 1):
                for d in (0, 1):
                    copy(j, m, d).wait_send()


def per_device(tokens, gate_weight, up_weight, down_weight, gate_mask, up_mask, down_mask):
    own, k = tokens.shape
    ff = gate_weight.shape[1]
    n = down_weight.shape[1]
    cw = ff // ROUNDS
    vmem, dma = pltpu.VMEM, pltpu.SemaphoreType.DMA
    anywhere = pl.BlockSpec(memory_space=pl.ANY)
    scalars = pl.BlockSpec(memory_space=pltpu.SMEM)
    return pl.pallas_call(
        layer_kernel,
        out_shape=jax.ShapeDtypeStruct((own, n), BF16),
        in_specs=[anywhere] * 4 + [scalars] * 3,
        out_specs=pl.BlockSpec(memory_space=pltpu.VMEM),
        scratch_shapes=[
            vmem((4, 4, 64, k), BF16),
            vmem((ROUNDS, k, cw), BF16),
            vmem((ROUNDS, k, cw), BF16),
            vmem((ROUNDS, cw, n), BF16),
            vmem((ROUNDS, 2, 3, 4, 64, cw), BF16),
            vmem((ROUNDS, 2, 2, 2, 64, cw), BF16),
            vmem((ROUNDS, 2, 2, 4, 64, cw), BF16),
            vmem((4, 2, 4, 64, cw), F32),
            vmem((ROUNDS, 2, 3, 64, cw), BF16),
            vmem((ROUNDS, 2, 2, 32, cw), BF16),
            vmem((ROUNDS, 2, 2, 64, cw), BF16),
            vmem((ROUNDS, 2, 4, 4, 64, cw // 2), BF16),
            vmem((8, own, n), F32),
            vmem((4, own, n), BF16),
            vmem((4, own, n), BF16),
            vmem((3, own, n), BF16),
            vmem((2, own // 2, n), BF16),
            vmem((2, own, n), BF16),
            dma((4, ROUNDS)),
            dma((8,)),
            dma((8,)),
            dma((16, ROUNDS)),
            dma((16, ROUNDS)),
            dma((16, ROUNDS)),
            dma((16, ROUNDS)),
            dma((8,)),
            dma((8,)),
        ],
        compiler_params=pltpu.CompilerParams(
            collective_id=0, has_side_effects=True, vmem_limit_bytes=67_043_328
        ),
    )(tokens.reshape(2, own // 2, k), gate_weight, up_weight, down_weight, gate_mask, up_mask, down_mask)


def solution(mesh):
    return jax.shard_map(
        per_device,
        mesh=mesh,
        in_specs=(
            P("row", "col"),
            P("col", "row"),
            P("col", "row"),
            P("row", "col"),
            P("col", "row"),
            P("col", "row"),
            P("row", "col"),
        ),
        out_specs=P("row", "col"),
        check_vma=False,
    )
```

```python
import jax
import jax.numpy as jnp
from jax import lax
from jax.experimental import pallas as pl
from jax.experimental.pallas import tpu as pltpu
from jax.sharding import PartitionSpec as P

BLOCK = 128
ROUNDS = 7
F32, BF16 = jnp.float32, jnp.bfloat16
MESH = pl.DeviceIdType.MESH
STEP = (1, -1)


def layer_kernel(
    tok_hbm, gate_hbm, up_hbm, down_hbm, gm, um, dm, out_ref,
    tok, w_own, w_out, w_in, w_down,
    s1, r1, part, s2, r2h, r2f, hid, acc, o_send, o_recv, oy_send, oy_h, oy_f,
    load_sem, down_sem, tok_load, tok_ss, tok_rs, twin_ss, twin_rs, w_ss, w_rs, rs_ss, rs_rs, ag_ss, ag_rs,
    out_ss, out_rs,
):
    row, col = lax.axis_index("row"), lax.axis_index("col")
    y, core = row // 2, row % 2
    x, z = col // 4, col % 4
    coord = (x, z)
    half = tuple(v // 2 for v in coord)
    kind = tuple(((v + 1) // 2) % 2 for v in coord)
    n = acc.shape[-1]

    def turn(v, k):
        return (v + k + 4) % 4

    def at(axis, v):
        return (row, v * 4 + z) if axis == 0 else (row, x * 4 + v)

    def in_plane(axis, k):
        return at(axis, turn(coord[axis], k))

    def odd(axis):
        return at(axis, coord[axis] + 1 - 2 * (coord[axis] % 2))

    def even(axis):
        return at(axis, 3 - coord[axis])

    def in_line(k):
        return (turn(y, k) * 2 + core, col)

    twin = (row + 1 - 2 * core, col)

    def remote(src, dst, ss, rs, device):
        return pltpu.make_async_remote_copy(
            src_ref=src, dst_ref=dst, send_sem=ss, recv_sem=rs, device_id=device, device_id_type=MESH
        )

    def block_of(t, c, j):
        return (2 * t + c) * ROUNDS + j

    def load_w(j, t, out, m):
        c = (1 - kind[t]) if out else kind[t]
        src = (up_hbm if m else gate_hbm).at[:, pl.ds(pl.multiple_of(block_of(t, c, j) * BLOCK, BLOCK), BLOCK)]
        dst = (w_out if out else w_own).at[j, t, :, pl.ds(m * BLOCK, BLOCK)]
        return pltpu.make_async_copy(src, dst, load_sem.at[t * 4 + out * 2 + m, j])

    def load_down(j, t, c):
        src = down_hbm.at[pl.ds(pl.multiple_of(block_of(t, c, j) * BLOCK, BLOCK), BLOCK)]
        return pltpu.make_async_copy(src, w_down.at[j, pl.ds((2 * t + c) * BLOCK, BLOCK)], down_sem.at[2 * t + c, j])

    load_tok = pltpu.make_async_copy(tok_hbm, tok.at[0, y, core], tok_load.at[0])
    load_tok.start()

    @pl.loop(0, ROUNDS)
    def _(j):
        for out in (1, 0):
            for t in (0, 1):
                for m in (0, 1):
                    load_w(j, t, out, m).start()

    @pl.loop(0, ROUNDS)
    def _(j):
        for t in (0, 1):
            for c in (0, 1):
                load_down(j, t, c).start()

    barrier = pltpu.get_barrier_semaphore()
    peers = [in_plane(a, k) for a in (0, 1) for k in STEP] + [in_line(k) for k in STEP] + [twin]
    for peer in peers:
        pl.semaphore_signal(barrier, inc=1, device_id=peer, device_id_type=MESH)
    pl.semaphore_wait(barrier, len(peers))

    def y_full(s, d):
        piece = tok.at[s, y, core]
        return remote(tok_hbm if s == 0 else piece, piece, tok_ss.at[2 * s + d], tok_rs.at[2 * s + d], in_line(STEP[d]))

    def y_half(d):
        piece = tok.at[0, turn(y, -STEP[d]), core, pl.ds(64 * d, 64)]
        return remote(piece, piece, tok_ss.at[6 + d], tok_rs.at[6 + d], in_line(STEP[d]))

    def odd_near(t):
        return remote(tok_hbm, tok.at[1 + t, y, core], tok_ss.at[8 + t], tok_rs.at[8 + t], odd(t))

    def odd_far(t):
        v = turn(y, 2)
        return remote(tok.at[0, v, core], tok.at[1 + t, v, core], tok_ss.at[10 + t], tok_rs.at[10 + t], odd(t))

    def to_twin(s, k):
        piece = tok.at[s, turn(y, k), core]
        return remote(piece, piece, twin_ss.at[s, k % 4], twin_rs.at[s, k % 4], twin)

    def send_w(j, t):
        return remote(w_out.at[j, t], w_in.at[j, t], w_ss.at[t, j], w_rs.at[t, j], odd(t))

    def prune(w, view, keep):
        keep = jnp.full((16, BLOCK), keep.astype(F32), F32).astype(BF16)
        w[view] = (w[view].reshape(BLOCK // 16, 16, BLOCK) * keep[None]).reshape(BLOCK, BLOCK)

    def stage_w(j):
        for out in (1, 0):
            w = w_out if out else w_own
            for t in (0, 1):
                c = (1 - kind[t]) if out else kind[t]
                for m in (0, 1):
                    load_w(j, t, out, m).wait()
                    for a in range(w.shape[2] // BLOCK):
                        view = (j, t, pl.ds(a * BLOCK, BLOCK), pl.ds(m * BLOCK, BLOCK))
                        prune(w, view, (um if m else gm)[a, block_of(t, c, j)])
                if out:
                    send_w(j, t).start()

    def rs1(j, t):
        return remote(s1.at[j, t], r1.at[j, t], rs_ss.at[t * 5, j], rs_rs.at[t * 5, j], even(t))

    def rs2h(j, t, d):
        k = t * 5 + 1 + d
        return remote(s2.at[j, t, 0, pl.ds(64 * d, 64)], r2h.at[j, t, d], rs_ss.at[k, j], rs_rs.at[k, j], in_plane(1 - t, STEP[d]))

    def rs2f(j, t, d):
        k = t * 5 + 3 + d
        return remote(s2.at[j, t, 1 + d], r2f.at[j, t, d], rs_ss.at[k, j], rs_rs.at[k, j], in_plane(1 - t, STEP[d]))

    def ag1f(j, t, d):
        k = t * 8 + d
        piece = hid.at[j, t, x, z]
        return remote(piece, piece, ag_ss.at[k, j], ag_rs.at[k, j], in_plane(t, STEP[d]))

    def ag1h(j, t, d):
        k = t * 8 + 2 + d
        rows = pl.ds(64 * d, 64)
        piece = hid.at[j, 0, turn(x, -STEP[d]), z, rows] if t == 0 else hid.at[j, 1, x, turn(z, -STEP[d]), rows]
        return remote(piece, piece, ag_ss.at[k, j], ag_rs.at[k, j], in_plane(t, STEP[d]))

    def ag2f(j, t, d):
        k = t * 8 + 4 + d
        piece = hid.at[j, 0, :, z] if t == 0 else hid.at[j, 1, x]
        return remote(piece, piece, ag_ss.at[k, j], ag_rs.at[k, j], in_plane(1 - t, STEP[d]))

    def ag2h(j, t, d):
        k = t * 8 + 6 + d
        rows = pl.ds(64 * d, 64)
        piece = hid.at[j, 0, :, turn(z, -STEP[d]), rows] if t == 0 else hid.at[j, 1, turn(x, -STEP[d]), :, rows]
        return remote(piece, piece, ag_ss.at[k, j], ag_rs.at[k, j], in_plane(1 - t, STEP[d]))

    def product(j, t, h):
        rows, k = pl.ds(2 * h, 2), tok.shape[-1]
        got = jnp.dot(tok[0, rows].reshape(512, k), w_own[j, t], preferred_element_type=F32)
        got = got + jnp.dot(tok[1 + t, rows].reshape(512, k), w_in[j, t], preferred_element_type=F32)
        return got.reshape(4, 128, 2 * BLOCK)

    def stage_a(j):
        for t in (0, 1):
            send_w(j, t).wait_recv()
            s1[j, t] = product(j, t, 1 - half[t]).astype(BF16)
            rs1(j, t).start()

    def stage_b(j):
        for t in (0, 1):
            got = product(j, t, half[t])
            rs1(j, t).wait_recv()
            part[j % 4, t] = got + r1[j, t].astype(F32)
            s2[j, t, 0] = part[j % 4, t, turn(coord[1 - t], 2)].astype(BF16)
            for d in (0, 1):
                rs2h(j, t, d).start()

    def stage_c(j):
        for t in (0, 1):
            for d in (0, 1):
                rs2h(j, t, d).wait_recv()
                got = part[j % 4, t, turn(coord[1 - t], STEP[d])]
                lo, hi = 64 * d, 64 - 64 * d
                s2[j, t, 1 + d, pl.ds(lo, 64)] = (got[lo : lo + 64] + r2h[j, t, d].astype(F32)).astype(BF16)
                s2[j, t, 1 + d, pl.ds(hi, 64)] = got[hi : hi + 64].astype(BF16)
                rs2f(j, t, d).start()

    def stage_d(j):
        for t in (0, 1):
            for d in (0, 1):
                rs2f(j, t, d).wait_recv()
            got = part[j % 4, t, coord[1 - t]] + r2f[j, t, 0].astype(F32) + r2f[j, t, 1].astype(F32)
            g, u = got[:, :BLOCK], got[:, BLOCK:]
            hid[j, t, x, z] = (g / (1.0 + jnp.exp(-g)) * u).astype(BF16)
            for d in (0, 1):
                ag1f(j, t, d).start()

    def relay(first, then):
        def stage(j):
            for t in (0, 1):
                for d in (0, 1):
                    first(j, t, d).wait_recv()
                    then(j, t, d).start()
        return stage

    def stage_f(j):
        for t in (0, 1):
            for d in (0, 1):
                ag1h(j, t, d).wait_recv()
            for d in (0, 1):
                ag2f(j, t, d).start()

    def stage_h(j):
        for t in (0, 1):
            for c in (0, 1):
                load_down(j, t, c).wait()
                for b in range(n // BLOCK):
                    prune(w_down, (j, pl.ds((2 * t + c) * BLOCK, BLOCK), pl.ds(b * BLOCK, BLOCK)), dm[b, block_of(t, c, j)])
        for t in (0, 1):
            for d in (0, 1):
                ag2h(j, t, d).wait_recv()
        for h, (first, second) in enumerate(((0, 1), (3, 2))):
            lhs = [hid[j, 0, first], hid[j, 0, second], hid[j, 1, :, first], hid[j, 1, :, second]]
            lhs = jnp.concatenate([v.reshape(512, BLOCK) for v in lhs], axis=1)
            got = jnp.dot(lhs, w_down[j], preferred_element_type=F32).reshape(4, 128, n)
            acc[pl.ds(4 * h, 4)] = acc[pl.ds(4 * h, 4)] + got

    for d in (0, 1):
        y_full(0, d).start()
    for t in (0, 1):
        odd_near(t).start()
    load_tok.wait()
    to_twin(0, 0).start()
    acc[...] = jnp.zeros_like(acc)
    stage_w(0)
    for d in (0, 1):
        y_full(0, d).wait_recv()
        y_half(d).start()
        to_twin(0, -STEP[d]).start()
    for t in (0, 1):
        odd_near(t).wait_recv()
        for d in (0, 1):
            y_full(1 + t, d).start()
        to_twin(1 + t, 0).start()
    for d in (0, 1):
        y_half(d).wait_recv()
    for t in (0, 1):
        odd_far(t).start()
    to_twin(0, 2).start()
    stage_w(1)
    for t in (0, 1):
        for d in (0, 1):
            y_full(1 + t, d).wait_recv()
            to_twin(1 + t, -STEP[d]).start()
    for t in (0, 1):
        odd_far(t).wait_recv()
        to_twin(1 + t, 2).start()
    for s in range(3):
        for k in range(4):
            to_twin(s, k).wait_recv()

    stages = (
        (stage_w, -2),
        (stage_a, 0),
        (stage_b, 1),
        (stage_c, 2),
        (stage_d, 3),
        (relay(ag1f, ag1h), 4),
        (stage_f, 5),
        (relay(ag2f, ag2h), 6),
        (stage_h, 7),
    )

    @pl.loop(0, ROUNDS + 7)
    def _(i):
        for stage, lag in stages:
            @pl.when((i >= lag) & (i < ROUNDS + lag))
            def _(stage=stage, lag=lag):
                stage(i - lag)

    def o_twin(k):
        return remote(o_send.at[k], o_recv.at[k], out_ss.at[k], out_rs.at[k], twin)

    def oyh(d):
        return remote(oy_send.at[0, pl.ds(64 * d, 64)], oy_h.at[d], out_ss.at[4 + d], out_rs.at[4 + d], in_line(STEP[d]))

    def oyf(d):
        return remote(oy_send.at[1 + d], oy_f.at[d], out_ss.at[6 + d], out_rs.at[6 + d], in_line(STEP[d]))

    for k in (2, 1, 3, 0):
        o_send[k] = acc[turn(y, k) * 2 + 1 - core].astype(BF16)
        o_twin(k).start()

    def paired(k):
        o_twin(k).wait_recv()
        return acc[turn(y, k) * 2 + core] + o_recv[k].astype(F32)

    oy_send[0] = paired(2).astype(BF16)
    for d in (0, 1):
        oyh(d).start()
    for d in (0, 1):
        got = paired(1 if d == 0 else 3)
        oyh(d).wait_recv()
        lo, hi = 64 * d, 64 - 64 * d
        oy_send[1 + d, pl.ds(lo, 64)] = (got[lo : lo + 64] + oy_h[d].astype(F32)).astype(BF16)
        oy_send[1 + d, pl.ds(hi, 64)] = got[hi : hi + 64].astype(BF16)
        oyf(d).start()
    got = paired(0)
    for d in (0, 1):
        oyf(d).wait_recv()
    out_ref[...] = (got + oy_f[0].astype(F32) + oy_f[1].astype(F32)).astype(BF16)

    for d in (0, 1):
        for s in range(3):
            y_full(s, d).wait_send()
        y_half(d).wait_send()
        odd_near(d).wait_send()
        odd_far(d).wait_send()
        oyh(d).wait_send()
        oyf(d).wait_send()
    for k in range(4):
        for s in range(3):
            to_twin(s, k).wait_send()
        o_twin(k).wait_send()

    @pl.loop(0, ROUNDS)
    def _(j):
        for t in (0, 1):
            send_w(j, t).wait_send()
            rs1(j, t).wait_send()
            for d in (0, 1):
                for copy in (rs2h, rs2f, ag1f, ag1h, ag2f, ag2h):
                    copy(j, t, d).wait_send()


def per_device(tokens, gate_weight, up_weight, down_weight, gate_mask, up_mask, down_mask):
    own, k = tokens.shape
    n = down_weight.shape[1]
    vmem, dma = pltpu.VMEM, pltpu.SemaphoreType.DMA
    anywhere = pl.BlockSpec(memory_space=pl.ANY)
    scalars = pl.BlockSpec(memory_space=pltpu.SMEM)
    return pl.pallas_call(
        layer_kernel,
        out_shape=jax.ShapeDtypeStruct((own, n), BF16),
        in_specs=[anywhere] * 4 + [scalars] * 3,
        out_specs=pl.BlockSpec(memory_space=pltpu.VMEM),
        scratch_shapes=[
            vmem((3, 4, 2, own, k), BF16),
            vmem((ROUNDS, 2, k, 2 * BLOCK), BF16),
            vmem((ROUNDS, 2, k, 2 * BLOCK), BF16),
            vmem((ROUNDS, 2, k, 2 * BLOCK), BF16),
            vmem((ROUNDS, 4 * BLOCK, n), BF16),
            vmem((ROUNDS, 2, 4, own, 2 * BLOCK), BF16),
            vmem((ROUNDS, 2, 4, own, 2 * BLOCK), BF16),
            vmem((4, 2, 4, own, 2 * BLOCK), F32),
            vmem((ROUNDS, 2, 3, own, 2 * BLOCK), BF16),
            vmem((ROUNDS, 2, 2, own // 2, 2 * BLOCK), BF16),
            vmem((ROUNDS, 2, 2, own, 2 * BLOCK), BF16),
            vmem((ROUNDS, 2, 4, 4, own, BLOCK), BF16),
            vmem((8, own, n), F32),
            vmem((4, own, n), BF16),
            vmem((4, own, n), BF16),
            vmem((3, own, n), BF16),
            vmem((2, own // 2, n), BF16),
            vmem((2, own, n), BF16),
            dma((8, ROUNDS)),
            dma((4, ROUNDS)),
            dma((1,)),
            dma((12,)),
            dma((12,)),
            dma((3, 4)),
            dma((3, 4)),
            dma((2, ROUNDS)),
            dma((2, ROUNDS)),
            dma((10, ROUNDS)),
            dma((10, ROUNDS)),
            dma((16, ROUNDS)),
            dma((16, ROUNDS)),
            dma((8,)),
            dma((8,)),
        ],
        compiler_params=pltpu.CompilerParams(
            collective_id=0, has_side_effects=True, vmem_limit_bytes=67_043_328
        ),
    )(tokens, gate_weight, up_weight, down_weight, gate_mask, up_mask, down_mask.T)


def solution(mesh):
    return jax.shard_map(
        per_device,
        mesh=mesh,
        in_specs=(
            P("row", "col"),
            P("col", "row"),
            P("col", "row"),
            P("row", "col"),
            P("col", "row"),
            P("col", "row"),
            P("row", "col"),
        ),
        out_specs=P("row", "col"),
        check_vma=False,
    )
```

```python
import jax
import jax.numpy as jnp
from jax import lax
from jax.experimental import pallas as pl
from jax.experimental.pallas import tpu as pltpu
from jax.sharding import PartitionSpec as P

BLOCK = 128
ROUNDS = 7
F32, BF16 = jnp.float32, jnp.bfloat16
MESH = pl.DeviceIdType.MESH
STEP = (1, -1)


def layer_kernel(
    tok_hbm, gate_hbm, up_hbm, down_hbm, gm, um, dm, out_ref,
    tok, w_own, w_out, w_in, w_down,
    s1, r1, part, s2, r2h, r2f, hid, acc, o_send, o_recv, oy_send, oy_h, oy_f,
    load_sem, down_sem, tok_load, tok_ss, tok_rs, twin_ss, twin_rs, w_ss, w_rs, rs_ss, rs_rs, ag_ss, ag_rs,
    out_ss, out_rs,
):
    row, col = lax.axis_index("row"), lax.axis_index("col")
    y, core = row // 2, row % 2
    x, z = col // 4, col % 4
    coord = (x, z)
    half = tuple(v // 2 for v in coord)
    kind = tuple(((v + 1) // 2) % 2 for v in coord)
    n = acc.shape[-1]

    def turn(v, k):
        return (v + k + 4) % 4

    def at(axis, v):
        return (row, v * 4 + z) if axis == 0 else (row, x * 4 + v)

    def in_plane(axis, k):
        return at(axis, turn(coord[axis], k))

    def odd(axis):
        return at(axis, coord[axis] + 1 - 2 * (coord[axis] % 2))

    def even(axis):
        return at(axis, 3 - coord[axis])

    def in_line(k):
        return (turn(y, k) * 2 + core, col)

    twin = (row + 1 - 2 * core, col)

    def remote(src, dst, ss, rs, device):
        return pltpu.make_async_remote_copy(
            src_ref=src, dst_ref=dst, send_sem=ss, recv_sem=rs, device_id=device, device_id_type=MESH
        )

    def block_of(t, c, j):
        return (2 * t + c) * ROUNDS + j

    def load_w(j, t, out, m):
        c = (1 - kind[t]) if out else kind[t]
        src = (up_hbm if m else gate_hbm).at[:, pl.ds(pl.multiple_of(block_of(t, c, j) * BLOCK, BLOCK), BLOCK)]
        dst = (w_out if out else w_own).at[j, t, :, pl.ds(m * BLOCK, BLOCK)]
        return pltpu.make_async_copy(src, dst, load_sem.at[t * 4 + out * 2 + m, j])

    def load_down(j, t, c):
        src = down_hbm.at[pl.ds(pl.multiple_of(block_of(t, c, j) * BLOCK, BLOCK), BLOCK)]
        return pltpu.make_async_copy(src, w_down.at[j, pl.ds((2 * t + c) * BLOCK, BLOCK)], down_sem.at[2 * t + c, j])

    load_tok = pltpu.make_async_copy(tok_hbm, tok.at[0, y, core], tok_load.at[0])
    load_tok.start()

    @pl.loop(0, ROUNDS)
    def _(j):
        for out in (1, 0):
            for t in (0, 1):
                for m in (0, 1):
                    load_w(j, t, out, m).start()

    @pl.loop(0, ROUNDS)
    def _(j):
        for t in (0, 1):
            for c in (0, 1):
                load_down(j, t, c).start()

    barrier = pltpu.get_barrier_semaphore()
    peers = [in_plane(a, k) for a in (0, 1) for k in STEP] + [in_line(k) for k in STEP] + [twin]
    for peer in peers:
        pl.semaphore_signal(barrier, inc=1, device_id=peer, device_id_type=MESH)
    pl.semaphore_wait(barrier, len(peers))

    def y_full(s, d):
        piece = tok.at[s, y, core]
        return remote(tok_hbm if s == 0 else piece, piece, tok_ss.at[2 * s + d], tok_rs.at[2 * s + d], in_line(STEP[d]))

    def y_half(d):
        piece = tok.at[0, turn(y, -STEP[d]), core, pl.ds(64 * d, 64)]
        return remote(piece, piece, tok_ss.at[6 + d], tok_rs.at[6 + d], in_line(STEP[d]))

    def odd_near(t):
        return remote(tok_hbm, tok.at[1 + t, y, core], tok_ss.at[8 + t], tok_rs.at[8 + t], odd(t))

    def odd_far(t):
        v = turn(y, 2)
        return remote(tok.at[0, v, core], tok.at[1 + t, v, core], tok_ss.at[10 + t], tok_rs.at[10 + t], odd(t))

    def to_twin(s, k):
        piece = tok.at[s, turn(y, k), core]
        return remote(piece, piece, twin_ss.at[s, k % 4], twin_rs.at[s, k % 4], twin)

    def send_w(j, t):
        return remote(w_out.at[j, t], w_in.at[j, t], w_ss.at[t, j], w_rs.at[t, j], odd(t))

    def prune(w, view, keep):
        keep = jnp.full((16, BLOCK), keep.astype(F32), F32).astype(BF16)
        w[view] = (w[view].reshape(BLOCK // 16, 16, BLOCK) * keep[None]).reshape(BLOCK, BLOCK)

    def stage_w(j):
        for out in (1, 0):
            w = w_out if out else w_own
            for t in (0, 1):
                c = (1 - kind[t]) if out else kind[t]
                for m in (0, 1):
                    load_w(j, t, out, m).wait()
                    for a in range(w.shape[2] // BLOCK):
                        view = (j, t, pl.ds(a * BLOCK, BLOCK), pl.ds(m * BLOCK, BLOCK))
                        prune(w, view, (um if m else gm)[a, block_of(t, c, j)])
                if out:
                    send_w(j, t).start()

    def rs1(j, t):
        return remote(s1.at[j, t], r1.at[j, t], rs_ss.at[t * 5, j], rs_rs.at[t * 5, j], even(t))

    def rs2h(j, t, d):
        k = t * 5 + 1 + d
        return remote(s2.at[j, t, 0, pl.ds(64 * d, 64)], r2h.at[j, t, d], rs_ss.at[k, j], rs_rs.at[k, j], in_plane(1 - t, STEP[d]))

    def rs2f(j, t, d):
        k = t * 5 + 3 + d
        return remote(s2.at[j, t, 1 + d], r2f.at[j, t, d], rs_ss.at[k, j], rs_rs.at[k, j], in_plane(1 - t, STEP[d]))

    def ag1f(j, t, d):
        k = t * 8 + d
        piece = hid.at[j, t, x, z]
        return remote(piece, piece, ag_ss.at[k, j], ag_rs.at[k, j], in_plane(t, STEP[d]))

    def ag1h(j, t, d):
        k = t * 8 + 2 + d
        rows = pl.ds(64 * d, 64)
        piece = hid.at[j, 0, turn(x, -STEP[d]), z, rows] if t == 0 else hid.at[j, 1, x, turn(z, -STEP[d]), rows]
        return remote(piece, piece, ag_ss.at[k, j], ag_rs.at[k, j], in_plane(t, STEP[d]))

    def ag2f(j, t, d):
        k = t * 8 + 4 + d
        piece = hid.at[j, 0, :, z] if t == 0 else hid.at[j, 1, x]
        return remote(piece, piece, ag_ss.at[k, j], ag_rs.at[k, j], in_plane(1 - t, STEP[d]))

    def ag2h(j, t, d):
        k = t * 8 + 6 + d
        rows = pl.ds(64 * d, 64)
        piece = hid.at[j, 0, :, turn(z, -STEP[d]), rows] if t == 0 else hid.at[j, 1, turn(x, -STEP[d]), :, rows]
        return remote(piece, piece, ag_ss.at[k, j], ag_rs.at[k, j], in_plane(1 - t, STEP[d]))

    def product(j, t, h):
        rows, k = pl.ds(2 * h, 2), tok.shape[-1]
        got = jnp.dot(tok[0, rows].reshape(512, k), w_own[j, t], preferred_element_type=F32)
        got = got + jnp.dot(tok[1 + t, rows].reshape(512, k), w_in[j, t], preferred_element_type=F32)
        return got.reshape(4, 128, 2 * BLOCK)

    def stage_a(j):
        for t in (0, 1):
            send_w(j, t).wait_recv()
            s1[j, t] = product(j, t, 1 - half[t]).astype(BF16)
            rs1(j, t).start()

    def stage_b(j):
        for t in (0, 1):
            got = product(j, t, half[t])
            rs1(j, t).wait_recv()
            part[j % 4, t] = got + r1[j, t].astype(F32)
            s2[j, t, 0] = part[j % 4, t, turn(coord[1 - t], 2)].astype(BF16)
            for d in (0, 1):
                rs2h(j, t, d).start()

    def stage_c(j):
        for t in (0, 1):
            for d in (0, 1):
                rs2h(j, t, d).wait_recv()
                got = part[j % 4, t, turn(coord[1 - t], STEP[d])]
                lo, hi = 64 * d, 64 - 64 * d
                s2[j, t, 1 + d, pl.ds(lo, 64)] = (got[lo : lo + 64] + r2h[j, t, d].astype(F32)).astype(BF16)
                s2[j, t, 1 + d, pl.ds(hi, 64)] = got[hi : hi + 64].astype(BF16)
                rs2f(j, t, d).start()

    def stage_d(j):
        for t in (0, 1):
            for d in (0, 1):
                rs2f(j, t, d).wait_recv()
            got = part[j % 4, t, coord[1 - t]] + r2f[j, t, 0].astype(F32) + r2f[j, t, 1].astype(F32)
            g, u = got[:, :BLOCK], got[:, BLOCK:]
            hid[j, t, x, z] = (g / (1.0 + jnp.exp(-g)) * u).astype(BF16)
            for d in (0, 1):
                ag1f(j, t, d).start()

    def relay(first, then):
        def stage(j):
            for t in (0, 1):
                for d in (0, 1):
                    first(j, t, d).wait_recv()
                    then(j, t, d).start()
        return stage

    def stage_f(j):
        for t in (0, 1):
            for d in (0, 1):
                ag1h(j, t, d).wait_recv()
            for d in (0, 1):
                ag2f(j, t, d).start()

    def ready(j):
        for t in (0, 1):
            for c in (0, 1):
                load_down(j, t, c).wait()
                for b in range(n // BLOCK):
                    prune(w_down, (j, pl.ds((2 * t + c) * BLOCK, BLOCK), pl.ds(b * BLOCK, BLOCK)), dm[b, block_of(t, c, j)])
        for t in (0, 1):
            for d in (0, 1):
                ag2h(j, t, d).wait_recv()

    def stage_h(j):
        ready(j)
        for h, (first, second) in enumerate(((0, 1), (3, 2))):
            lhs = [hid[j, 0, first], hid[j, 0, second], hid[j, 1, :, first], hid[j, 1, :, second]]
            lhs = jnp.concatenate([v.reshape(512, BLOCK) for v in lhs], axis=1)
            got = jnp.dot(lhs, w_down[j], preferred_element_type=F32).reshape(4, 128, n)
            acc[pl.ds(4 * h, 4)] = acc[pl.ds(4 * h, 4)] + got

    for d in (0, 1):
        y_full(0, d).start()
    for t in (0, 1):
        odd_near(t).start()
    load_tok.wait()
    to_twin(0, 0).start()
    acc[...] = jnp.zeros_like(acc)
    stage_w(0)
    for d in (0, 1):
        y_full(0, d).wait_recv()
        y_half(d).start()
        to_twin(0, -STEP[d]).start()
    for t in (0, 1):
        odd_near(t).wait_recv()
        for d in (0, 1):
            y_full(1 + t, d).start()
        to_twin(1 + t, 0).start()
    for d in (0, 1):
        y_half(d).wait_recv()
    for t in (0, 1):
        odd_far(t).start()
    to_twin(0, 2).start()
    stage_w(1)
    for t in (0, 1):
        for d in (0, 1):
            y_full(1 + t, d).wait_recv()
            to_twin(1 + t, -STEP[d]).start()
    for t in (0, 1):
        odd_far(t).wait_recv()
        to_twin(1 + t, 2).start()
    for s in range(3):
        for k in range(4):
            to_twin(s, k).wait_recv()

    stages = (
        (stage_w, -2),
        (stage_a, 0),
        (stage_b, 1),
        (stage_c, 2),
        (stage_d, 3),
        (relay(ag1f, ag1h), 4),
        (stage_f, 5),
        (relay(ag2f, ag2h), 6),
        (stage_h, 7),
    )

    @pl.loop(0, ROUNDS + 6)
    def _(i):
        for stage, lag in stages:
            @pl.when((i >= lag) & (i < ROUNDS + lag))
            def _(stage=stage, lag=lag):
                stage(i - lag)

    def o_twin(k):
        return remote(o_send.at[k], o_recv.at[k], out_ss.at[k], out_rs.at[k], twin)

    def oyh(d):
        return remote(oy_send.at[0, pl.ds(64 * d, 64)], oy_h.at[d], out_ss.at[4 + d], out_rs.at[4 + d], in_line(STEP[d]))

    def oyf(d):
        return remote(oy_send.at[1 + d], oy_f.at[d], out_ss.at[6 + d], out_rs.at[6 + d], in_line(STEP[d]))

    def last_product(k):
        j, v = ROUNDS - 1, turn(y, k)
        h, pair = v // 2, pl.ds(2 * (v % 2), 2)
        lhs = [hid[j, 0, 3 * h, pair], hid[j, 0, 1 + h, pair], hid[j, 1, pair, 3 * h], hid[j, 1, pair, 1 + h]]
        lhs = jnp.concatenate([p.reshape(256, BLOCK) for p in lhs], axis=1)
        got = jnp.dot(lhs, w_down[j], preferred_element_type=F32).reshape(2, 128, n)
        acc[pl.ds(2 * v, 2)] = acc[pl.ds(2 * v, 2)] + got
        o_send[k] = acc[2 * v + 1 - core].astype(BF16)
        o_twin(k).start()

    def paired(k):
        o_twin(k).wait_recv()
        return acc[turn(y, k) * 2 + core] + o_recv[k].astype(F32)

    ready(ROUNDS - 1)
    for k in (2, 1):
        last_product(k)
    oy_send[0] = paired(2).astype(BF16)
    for d in (0, 1):
        oyh(d).start()
    for k in (3, 0):
        last_product(k)
    for d in (0, 1):
        got = paired(1 if d == 0 else 3)
        oyh(d).wait_recv()
        lo, hi = 64 * d, 64 - 64 * d
        oy_send[1 + d, pl.ds(lo, 64)] = (got[lo : lo + 64] + oy_h[d].astype(F32)).astype(BF16)
        oy_send[1 + d, pl.ds(hi, 64)] = got[hi : hi + 64].astype(BF16)
        oyf(d).start()
    got = paired(0)
    for d in (0, 1):
        oyf(d).wait_recv()
    out_ref[...] = (got + oy_f[0].astype(F32) + oy_f[1].astype(F32)).astype(BF16)

    for d in (0, 1):
        for s in range(3):
            y_full(s, d).wait_send()
        y_half(d).wait_send()
        odd_near(d).wait_send()
        odd_far(d).wait_send()
        oyh(d).wait_send()
        oyf(d).wait_send()
    for k in range(4):
        for s in range(3):
            to_twin(s, k).wait_send()
        o_twin(k).wait_send()

    @pl.loop(0, ROUNDS)
    def _(j):
        for t in (0, 1):
            send_w(j, t).wait_send()
            rs1(j, t).wait_send()
            for d in (0, 1):
                for copy in (rs2h, rs2f, ag1f, ag1h, ag2f, ag2h):
                    copy(j, t, d).wait_send()


def per_device(tokens, gate_weight, up_weight, down_weight, gate_mask, up_mask, down_mask):
    own, k = tokens.shape
    n = down_weight.shape[1]
    vmem, dma = pltpu.VMEM, pltpu.SemaphoreType.DMA
    anywhere = pl.BlockSpec(memory_space=pl.ANY)
    scalars = pl.BlockSpec(memory_space=pltpu.SMEM)
    return pl.pallas_call(
        layer_kernel,
        out_shape=jax.ShapeDtypeStruct((own, n), BF16),
        in_specs=[anywhere] * 4 + [scalars] * 3,
        out_specs=pl.BlockSpec(memory_space=pltpu.VMEM),
        scratch_shapes=[
            vmem((3, 4, 2, own, k), BF16),
            vmem((ROUNDS, 2, k, 2 * BLOCK), BF16),
            vmem((ROUNDS, 2, k, 2 * BLOCK), BF16),
            vmem((ROUNDS, 2, k, 2 * BLOCK), BF16),
            vmem((ROUNDS, 4 * BLOCK, n), BF16),
            vmem((ROUNDS, 2, 4, own, 2 * BLOCK), BF16),
            vmem((ROUNDS, 2, 4, own, 2 * BLOCK), BF16),
            vmem((4, 2, 4, own, 2 * BLOCK), F32),
            vmem((ROUNDS, 2, 3, own, 2 * BLOCK), BF16),
            vmem((ROUNDS, 2, 2, own // 2, 2 * BLOCK), BF16),
            vmem((ROUNDS, 2, 2, own, 2 * BLOCK), BF16),
            vmem((ROUNDS, 2, 4, 4, own, BLOCK), BF16),
            vmem((8, own, n), F32),
            vmem((4, own, n), BF16),
            vmem((4, own, n), BF16),
            vmem((3, own, n), BF16),
            vmem((2, own // 2, n), BF16),
            vmem((2, own, n), BF16),
            dma((8, ROUNDS)),
            dma((4, ROUNDS)),
            dma((1,)),
            dma((12,)),
            dma((12,)),
            dma((3, 4)),
            dma((3, 4)),
            dma((2, ROUNDS)),
            dma((2, ROUNDS)),
            dma((10, ROUNDS)),
            dma((10, ROUNDS)),
            dma((16, ROUNDS)),
            dma((16, ROUNDS)),
            dma((8,)),
            dma((8,)),
        ],
        compiler_params=pltpu.CompilerParams(
            collective_id=0, has_side_effects=True, vmem_limit_bytes=67_043_328
        ),
    )(tokens, gate_weight, up_weight, down_weight, gate_mask, up_mask, down_mask.T)


def solution(mesh):
    return jax.shard_map(
        per_device,
        mesh=mesh,
        in_specs=(
            P("row", "col"),
            P("col", "row"),
            P("col", "row"),
            P("row", "col"),
            P("col", "row"),
            P("col", "row"),
            P("row", "col"),
        ),
        out_specs=P("row", "col"),
        check_vma=False,
    )
```
